256 devices in a mesh: tile: 8 (over x_lo, y), atom: 32 (over z, x_hi, core).
Axes of the slice: x: 4 (x_hi: 2, x_lo: 2; x = x_hi * 2 + x_lo), y: 4, z: 8, core: 2. Of those that a mesh axis runs over, the one named last changes fastest.
Arguments:
- observed: float32 [16, 128, 128], P(None, 'tile'), may hold values from -6 to 6
- coefficients: float32 [512, 128, 128], P('atom', 'tile'), may hold values from -6 to 6
- dictionary: float32 [512, 16, 8, 8], P('atom'), may hold values from -0.0078125 to 0.0078125
- thresholds: float32 [512], P('atom'), may hold values from 0.0125 to 0.125
Outputs:
- coded: float32 [512, 128, 128], P('atom', 'tile')
- misfit: float32 [16, 128, 128], P(None, 'tile')
The draws below stay inside these ranges and needn't reach their ends.
All inputs are finite; a program needn't handle non-finite values.
Results may differ from the reference program's by a relative error of at most 0.00015.
Values sent between devices are 32-bit elements; how exact they have to be, the bound alone decides.
No kernel may reach another device: no remote copies, remote signals or barrier semaphores. Data moves between devices by JAX's collectives and lax.ppermute only.
A program may use at most 64 MiB of HBM per device.

```python
import math
import jax
import jax.numpy as jnp
from jax import lax

C = 16
KS = 8
TW = 128
STEPS = 2
K = 512
H = 128


def shard_levels(stream_key, shape, shards, smallest, top_value):
    def one(dim, shards_of):
        steps = jax.random.uniform(jax.random.fold_in(jax.random.fold_in(stream_key, 6), dim), (shards_of,), jnp.float32, smallest / len(shards), top_value / len(shards))
        return jnp.repeat(jnp.exp(steps), shape[dim] // shards_of).reshape((-1,) + (1,) * (len(shape) - dim - 1))

    loudness = one(*shards[0])
    for cut in shards[1:]:
        loudness = loudness * one(*cut)
    return loudness


def gaussian(own_key, dims, spread, most, pieces=(), kind=jnp.bfloat16):
    values = jax.random.normal(own_key, dims, jnp.float32) * spread
    if len(pieces) > 0:
        values = shard_levels(own_key, dims, pieces, -0.22, 0.18) * values
    return jnp.clip(values, min=-most, max=most).astype(kind)


def setup_inputs(seed: int = 0) -> dict:
    splits = jax.random.split(jax.random.key(seed), 5)
    observed = gaussian(splits[0], (C, H, TW), 1.0, 6.0, ((1, 8),), jnp.float32)
    coefficients = gaussian(splits[1], (K, H, TW), 1.0, 6.0, ((0, 32), (1, 8)), jnp.float32)
    dictionary = gaussian(splits[2], (K, C, KS, KS), (K * C * KS * KS) ** -0.5, 0.0078125, ((0, 32),), jnp.float32)
    thresholds = jnp.clip(jnp.exp(math.log(0.125) - 2.3025851 * jax.random.uniform(splits[3], (K,), jnp.float32) ** shard_levels(splits[3], (K,), ((0, 32),), -0.2, 0.2)), 0.0125, 0.125)
    return {"observed": observed, "coefficients": coefficients, "dictionary": dictionary, "thresholds": thresholds}


step_size = 8.0


def synthesize(coeffs_now, dictionary):
    flipped = jnp.transpose(dictionary, (1, 0, 2, 3))[:, :, ::-1, ::-1]
    rim_rows = KS - 1
    result = lax.conv_general_dilated(coeffs_now[None], flipped, (1, 1), ((rim_rows, 0), (rim_rows, 0)), dimension_numbers=("NCHW", "OIHW", "NCHW"), precision=lax.Precision.HIGHEST)
    return result[0]


def correlate(residual, dictionary):
    rim_rows = KS - 1
    result = lax.conv_general_dilated(residual[None], dictionary, (1, 1), ((0, rim_rows), (0, rim_rows)), dimension_numbers=("NCHW", "OIHW", "NCHW"), precision=lax.Precision.HIGHEST)
    return result[0]


def reference(observed, coefficients, dictionary, thresholds):
    coeffs_now = coefficients
    misfit = observed
    for iteration in range(STEPS):
        misfit = synthesize(coeffs_now, dictionary) - observed
        stepped = coeffs_now - step_size * correlate(misfit, dictionary)
        cutoff = (step_size * thresholds)[:, None, None]
        coeffs_now = stepped - jnp.clip(stepped, -cutoff, cutoff)
    return coeffs_now, misfit
```

```python
import jax
import jax.numpy as jnp
from jax import lax
from jax.experimental import pallas as pl
from jax.experimental.pallas import tpu as pltpu
from jax.sharding import PartitionSpec as P

STEP = 8.0
KS = 8
ROWS = 16
CH = 16
TW = 128


def split(x):
    hi = x.astype(jnp.bfloat16)
    lo = (x - hi.astype(jnp.float32)).astype(jnp.bfloat16)
    return hi, lo


def stacked(w_ref):
    hi, lo = split(w_ref[...])
    return jnp.concatenate(
        [jnp.concatenate([hi, hi], axis=1), jnp.concatenate([lo, lo], axis=1)], axis=0
    )


def products(w, hi_ref, lo_ref, first, count):
    out = []
    for i in range(0, count, 2):
        pair = min(2, count - i)
        window = [
            jnp.concatenate(
                [
                    ref[first + i + d : first + i + d + KS].reshape(KS * CH, TW)
                    for ref in (hi_ref, lo_ref)
                ],
                axis=0,
            )
            for d in range(pair)
        ]
        x = jnp.concatenate(window, axis=1) if pair == 2 else window[0]
        q = jnp.dot(w, x, preferred_element_type=jnp.float32)
        q = q[: KS * CH] + q[KS * CH :]
        for d in range(pair):
            out.append(q[:, d * TW : (d + 1) * TW])
    return out


def gathered(q, lane, right):
    total = q[:CH]
    for b in range(1, KS):
        part = pltpu.roll(q[b * CH : (b + 1) * CH], b if right else TW - b, 1)
        keep = lane >= b if right else lane < TW - b
        total = total + jnp.where(keep, part, 0.0)
    return total


def lanes():
    return lax.broadcasted_iota(jnp.int32, (CH, TW), 1)


def synthesize(w, hi_ref, lo_ref, mine_ref, theirs_ref):
    lane = lanes()
    for i, q in enumerate(products(w, hi_ref, lo_ref, 1, ROWS)):
        s = gathered(q, lane, True)
        mine_ref[i] = s[: CH // 2]
        theirs_ref[i] = s[CH // 2 :]


def first_kernel(z_ref, zh_ref, ws_ref, mine_ref, theirs_ref, hi_ref, lo_ref):
    w = stacked(ws_ref)
    for r in range(8):
        hi_ref[r], lo_ref[r] = split(zh_ref[pl.ds(r, CH, stride=8), :])
    for r in range(ROWS):
        hi_ref[8 + r], lo_ref[8 + r] = split(z_ref[pl.ds(r, CH, stride=ROWS), :])
    synthesize(w, hi_ref, lo_ref, mine_ref, theirs_ref)


def load_misfit(mine_ref, theirs_ref, hi_ref, lo_ref, count):
    for r in range(count):
        hi_ref[r], lo_ref[r] = split(
            jnp.concatenate([mine_ref[r], theirs_ref[r]], axis=0)
        )


def second_kernel(
    inside_ref, z_ref, zh_ref, m_ref, t_ref, cut_ref, wr_ref, ws_ref,
    z1_ref, mine_ref, theirs_ref, mhi_ref, mlo_ref, zhi_ref, zlo_ref,
):
    wr = stacked(wr_ref)
    load_misfit(m_ref, t_ref, mhi_ref, mlo_ref, 32)
    lane = lanes()
    cut = cut_ref[...]
    inside = inside_ref[0]
    for n, q in enumerate(products(wr, mhi_ref, mlo_ref, 1, ROWS + KS - 1)):
        i = n - (KS - 1)
        r = gathered(q, lane, False)
        if i < 0:
            z = zh_ref[pl.ds(i + 8, CH, stride=8), :]
        else:
            z = z_ref[pl.ds(i, CH, stride=ROWS), :]
        moved = z - STEP * r
        z = moved - jnp.clip(moved, -cut, cut)
        if i < 0:
            z = jnp.where(inside > 0, z, 0.0)
        else:
            z1_ref[i] = z
        zhi_ref[8 + i], zlo_ref[8 + i] = split(z)
    synthesize(stacked(ws_ref), zhi_ref, zlo_ref, mine_ref, theirs_ref)


def third_kernel(
    core_ref, z_ref, m_ref, t_ref, cut_ref, wr_ref, coded_ref, misfit_ref, hi_ref, lo_ref
):
    wr = stacked(wr_ref)
    load_misfit(m_ref, t_ref, hi_ref, lo_ref, ROWS + 8)
    lane = lanes()
    cut = cut_ref[...]
    own = core_ref[0] == 0
    for i in range(ROWS):
        m, t = m_ref[i], t_ref[i]
        misfit_ref[pl.ds(i, 8, stride=ROWS), :] = jnp.where(own, m, t)
        misfit_ref[pl.ds(8 * ROWS + i, 8, stride=ROWS), :] = jnp.where(own, t, m)
    for i, q in enumerate(products(wr, hi_ref, lo_ref, 0, ROWS)):
        moved = z_ref[i] - STEP * gathered(q, lane, False)
        z = moved - jnp.clip(moved, -cut, cut)
        coded_ref[pl.ds(i, CH, stride=ROWS), :] = z


VMEM = pl.BlockSpec(memory_space=pltpu.VMEM)
SMEM = pl.BlockSpec(memory_space=pltpu.SMEM)


def f32(*shape):
    return jax.ShapeDtypeStruct(shape, jnp.float32)


def bf16(rows):
    return pltpu.VMEM((rows, CH, TW), jnp.bfloat16)


def call(kernel, in_specs, outs, scratch, flops):
    return pl.pallas_call(
        kernel,
        in_specs=in_specs,
        out_specs=[VMEM] * len(outs),
        out_shape=outs,
        scratch_shapes=scratch,
        cost_estimate=pl.CostEstimate(
            flops=flops, bytes_accessed=1 << 20, transcendentals=0
        ),
    )


def exchange(x, mask):
    pairs = [(i, i ^ mask) for i in range(lax.axis_size("atom"))]
    return lax.ppermute(x, "atom", pairs)


def summed(mine, theirs):
    total = mine + exchange(theirs, 1)
    for mask in (2, 4, 8, 28):
        total = total + exchange(total, mask)
    return total


def shifted(x, by):
    n = lax.axis_size("tile")
    return lax.ppermute(x, "tile", [(i, i + by) for i in range(n) if 0 <= i + by < n])


def per_device(observed, coefficients, dictionary, thresholds):
    core = lax.axis_index("atom") % 2
    tile = lax.axis_index("tile")
    half = CH // 2
    zh = shifted(coefficients[:, 8:, :], 1).reshape(CH * 8, TW)
    z0 = coefficients.reshape(CH * ROWS, TW)
    rolled = jnp.where(
        core == 0, dictionary, jnp.concatenate([dictionary[:, half:], dictionary[:, :half]], axis=1)
    )
    ws = jnp.transpose(rolled[:, :, ::-1, :], (3, 1, 2, 0)).reshape(KS * CH, KS * CH)
    wr = jnp.transpose(rolled, (3, 0, 2, 1)).reshape(KS * CH, KS * CH)
    cut = jnp.broadcast_to((STEP * thresholds)[:, None], (CH, TW))
    obs = jnp.transpose(
        jnp.where(core == 0, observed[:half], observed[half:]), (1, 0, 2)
    )
    core_id = core.astype(jnp.int32).reshape(1)
    inside = tile.astype(jnp.int32).reshape(1)
    part = f32(ROWS, half, TW)

    mine, theirs = call(
        first_kernel, [VMEM] * 3, [part, part], [bf16(24), bf16(24)], 1 << 29
    )(z0, zh, ws)
    misfit = summed(mine, theirs) - obs
    above = shifted(misfit[8:], 1)
    below = shifted(misfit[:8], -1)
    m = jnp.concatenate([above, misfit, below], axis=0)
    t = exchange(m, 1)
    z1, mine, theirs = call(
        second_kernel,
        [SMEM] + [VMEM] * 7,
        [f32(ROWS, CH, TW), part, part],
        [bf16(32), bf16(32), bf16(24), bf16(24)],
        1 << 30,
    )(inside, z0, zh, m, t, cut, wr, ws)
    misfit = summed(mine, theirs) - obs
    below = shifted(misfit[:8], -1)
    m = jnp.concatenate([misfit, below], axis=0)
    t = exchange(m, 1)
    coded, out = call(
        third_kernel,
        [SMEM] + [VMEM] * 5,
        [f32(CH * ROWS, TW), f32(CH * ROWS, TW)],
        [bf16(24), bf16(24)],
        1 << 29,
    )(core_id, z1, m, t, cut, wr)
    return coded.reshape(CH, ROWS, TW), out.reshape(CH, ROWS, TW)


def solution(mesh):
    in_specs = (
        P(None, "tile", None),
        P("atom", "tile", None),
        P("atom", None, None, None),
        P("atom"),
    )
    out_specs = (P("atom", "tile", None), P(None, "tile", None))
    return jax.shard_map(
        per_device, mesh=mesh, in_specs=in_specs, out_specs=out_specs, check_vma=False
    )
```

```python
import jax
import jax.numpy as jnp
from jax import lax
from jax.experimental import pallas as pl
from jax.experimental.pallas import tpu as pltpu
from jax.sharding import PartitionSpec as P

STEP = 8.0
KS = 8
ROWS = 16
CH = 16
TW = 128


def split(x):
    hi = x.astype(jnp.bfloat16)
    lo = (x - hi.astype(jnp.float32)).astype(jnp.bfloat16)
    return hi, lo


def stacked(w_ref):
    hi, lo = split(w_ref[...])
    return jnp.concatenate(
        [jnp.concatenate([hi, hi], axis=1), jnp.concatenate([lo, lo], axis=1)], axis=0
    )


def products(w, hi_ref, lo_ref, first, count):
    out = []
    for i in range(0, count, 2):
        pair = min(2, count - i)
        window = [
            jnp.concatenate(
                [
                    ref[first + i + d : first + i + d + KS].reshape(KS * CH, TW)
                    for ref in (hi_ref, lo_ref)
                ],
                axis=0,
            )
            for d in range(pair)
        ]
        x = jnp.concatenate(window, axis=1) if pair == 2 else window[0]
        q = jnp.dot(w, x, preferred_element_type=jnp.float32)
        q = q[: KS * CH] + q[KS * CH :]
        for d in range(pair):
            out.append(q[:, d * TW : (d + 1) * TW])
    return out


def gathered(q, lane, right):
    total = q[:CH]
    for b in range(1, KS):
        part = pltpu.roll(q[b * CH : (b + 1) * CH], b if right else TW - b, 1)
        keep = lane >= b if right else lane < TW - b
        total = total + jnp.where(keep, part, 0.0)
    return total


def lanes():
    return lax.broadcasted_iota(jnp.int32, (CH, TW), 1)


def synthesize(w, hi_ref, lo_ref, mine_ref, theirs_ref):
    lane = lanes()
    for i, q in enumerate(products(w, hi_ref, lo_ref, 1, ROWS)):
        s = gathered(q, lane, True)
        mine_ref[i] = s[: CH // 2]
        theirs_ref[i] = s[CH // 2 :]


def first_kernel(z_ref, zh_ref, ws_ref, mine_ref, theirs_ref, hi_ref, lo_ref):
    w = stacked(ws_ref)
    for r in range(8):
        hi_ref[r], lo_ref[r] = split(zh_ref[pl.ds(r, CH, stride=8), :])
    for r in range(ROWS):
        hi_ref[8 + r], lo_ref[8 + r] = split(z_ref[pl.ds(r, CH, stride=ROWS), :])
    synthesize(w, hi_ref, lo_ref, mine_ref, theirs_ref)


def load_misfit(mine_ref, theirs_ref, hi_ref, lo_ref, count):
    for r in range(count):
        hi_ref[r], lo_ref[r] = split(
            jnp.concatenate([mine_ref[r], theirs_ref[r]], axis=0)
        )


def second_kernel(
    inside_ref, z_ref, zh_ref, m_ref, t_ref, cut_ref, wr_ref, ws_ref,
    z1_ref, mine_ref, theirs_ref, mhi_ref, mlo_ref, zhi_ref, zlo_ref,
):
    wr = stacked(wr_ref)
    load_misfit(m_ref, t_ref, mhi_ref, mlo_ref, 32)
    lane = lanes()
    cut = cut_ref[...]
    inside = inside_ref[0]
    for n, q in enumerate(products(wr, mhi_ref, mlo_ref, 1, ROWS + KS - 1)):
        i = n - (KS - 1)
        r = gathered(q, lane, False)
        if i < 0:
            z = zh_ref[pl.ds(i + 8, CH, stride=8), :]
        else:
            z = z_ref[pl.ds(i, CH, stride=ROWS), :]
        moved = z - STEP * r
        z = moved - jnp.clip(moved, -cut, cut)
        if i < 0:
            z = jnp.where(inside > 0, z, 0.0)
        else:
            z1_ref[i] = z
        zhi_ref[8 + i], zlo_ref[8 + i] = split(z)
    synthesize(stacked(ws_ref), zhi_ref, zlo_ref, mine_ref, theirs_ref)


def third_kernel(
    core_ref, z_ref, m_ref, t_ref, cut_ref, wr_ref, coded_ref, misfit_ref, hi_ref, lo_ref
):
    wr = stacked(wr_ref)
    load_misfit(m_ref, t_ref, hi_ref, lo_ref, ROWS + 8)
    lane = lanes()
    cut = cut_ref[...]
    own = core_ref[0] == 0
    for i in range(ROWS):
        m, t = m_ref[i], t_ref[i]
        misfit_ref[pl.ds(i, 8, stride=ROWS), :] = jnp.where(own, m, t)
        misfit_ref[pl.ds(8 * ROWS + i, 8, stride=ROWS), :] = jnp.where(own, t, m)
    for i, q in enumerate(products(wr, hi_ref, lo_ref, 0, ROWS)):
        moved = z_ref[i] - STEP * gathered(q, lane, False)
        z = moved - jnp.clip(moved, -cut, cut)
        coded_ref[pl.ds(i, CH, stride=ROWS), :] = z


VMEM = pl.BlockSpec(memory_space=pltpu.VMEM)
SMEM = pl.BlockSpec(memory_space=pltpu.SMEM)


def f32(*shape):
    return jax.ShapeDtypeStruct(shape, jnp.float32)


def bf16(rows):
    return pltpu.VMEM((rows, CH, TW), jnp.bfloat16)


def call(kernel, in_specs, outs, scratch, flops):
    return pl.pallas_call(
        kernel,
        in_specs=in_specs,
        out_specs=[VMEM] * len(outs),
        out_shape=outs,
        scratch_shapes=scratch,
        compiler_params=pltpu.CompilerParams(vmem_limit_bytes=16 << 20),
        cost_estimate=pl.CostEstimate(
            flops=flops, bytes_accessed=1 << 20, transcendentals=0
        ),
    )


def exchange(x, mask):
    pairs = [(i, i ^ mask) for i in range(lax.axis_size("atom"))]
    return lax.ppermute(x, "atom", pairs)


def summed(mine, theirs):
    total = mine + exchange(theirs, 1)
    for mask in (2, 4, 8, 28):
        total = total + exchange(total, mask)
    return total


def shifted(x, by):
    n = lax.axis_size("tile")
    return lax.ppermute(x, "tile", [(i, i + by) for i in range(n) if 0 <= i + by < n])


def per_device(observed, coefficients, dictionary, thresholds):
    core = lax.axis_index("atom") % 2
    tile = lax.axis_index("tile")
    half = CH // 2
    zh = shifted(coefficients[:, 8:, :], 1).reshape(CH * 8, TW)
    z0 = coefficients.reshape(CH * ROWS, TW)
    rolled = jnp.where(
        core == 0, dictionary, jnp.concatenate([dictionary[:, half:], dictionary[:, :half]], axis=1)
    )
    ws = jnp.transpose(rolled[:, :, ::-1, :], (3, 1, 2, 0)).reshape(KS * CH, KS * CH)
    wr = jnp.transpose(rolled, (3, 0, 2, 1)).reshape(KS * CH, KS * CH)
    cut = jnp.broadcast_to((STEP * thresholds)[:, None], (CH, TW))
    obs = jnp.transpose(
        jnp.where(core == 0, observed[:half], observed[half:]), (1, 0, 2)
    )
    core_id = core.astype(jnp.int32).reshape(1)
    inside = tile.astype(jnp.int32).reshape(1)
    part = f32(ROWS, half, TW)

    mine, theirs = call(
        first_kernel, [VMEM] * 3, [part, part], [bf16(24), bf16(24)], 1 << 29
    )(z0, zh, ws)
    misfit = summed(mine, theirs) - obs
    above = shifted(misfit[8:], 1)
    below = shifted(misfit[:8], -1)
    m = jnp.concatenate([above, misfit, below], axis=0)
    t = exchange(m, 1)
    z1, mine, theirs = call(
        second_kernel,
        [SMEM] + [VMEM] * 7,
        [f32(ROWS, CH, TW), part, part],
        [bf16(32), bf16(32), bf16(24), bf16(24)],
        1 << 30,
    )(inside, z0, zh, m, t, cut, wr, ws)
    misfit = summed(mine, theirs) - obs
    below = shifted(misfit[:8], -1)
    m = jnp.concatenate([misfit, below], axis=0)
    t = exchange(m, 1)
    coded, out = call(
        third_kernel,
        [SMEM] + [VMEM] * 5,
        [f32(CH * ROWS, TW), f32(CH * ROWS, TW)],
        [bf16(24), bf16(24)],
        1 << 29,
    )(core_id, z1, m, t, cut, wr)
    return coded.reshape(CH, ROWS, TW), out.reshape(CH, ROWS, TW)


def solution(mesh):
    in_specs = (
        P(None, "tile", None),
        P("atom", "tile", None),
        P("atom", None, None, None),
        P("atom"),
    )
    out_specs = (P("atom", "tile", None), P(None, "tile", None))
    return jax.shard_map(
        per_device, mesh=mesh, in_specs=in_specs, out_specs=out_specs, check_vma=False
    )
```

```python
import jax
import jax.numpy as jnp
from jax import lax
from jax.experimental import pallas as pl
from jax.experimental.pallas import tpu as pltpu
from jax.sharding import PartitionSpec as P

STEP = 8.0
KS = 8
RIM = KS - 1
ROWS = 16
CH = 16
HALF = CH // 2
TW = 128
TAPS = KS * CH
EXT = ROWS + RIM
PARTNER = 0
BUTTERFLY = (2, 4, 8, 24)


def split(x):
    hi = x.astype(jnp.bfloat16)
    lo = (x - hi.astype(jnp.float32)).astype(jnp.bfloat16)
    return hi, lo


def stacked(hi, lo):
    return jnp.concatenate(
        [jnp.concatenate([hi, hi], axis=1), jnp.concatenate([lo, lo], axis=1)], axis=0
    )


def weights(refs, axis):
    return stacked(*split(jnp.concatenate([ref[...] for ref in refs], axis=axis)))


def products(w, sources, first, count):
    out = []
    half = w.shape[0] // 2
    for i in range(0, count, 2):
        pair = min(2, count - i)
        window = [
            jnp.concatenate(
                [
                    ref[first + i + d : first + i + d + KS].reshape(TAPS, TW)
                    for ref in sources
                ],
                axis=0,
            )
            for d in range(pair)
        ]
        x = jnp.concatenate(window, axis=1) if pair == 2 else window[0]
        q = jnp.dot(w, x, preferred_element_type=jnp.float32)
        q = q[:half] + q[half:]
        for d in range(pair):
            out.append(q[:, d * TW : (d + 1) * TW])
    return out


def gathered(q, lane, right):
    total = q[:CH]
    for b in range(1, KS):
        part = pltpu.roll(q[b * CH : (b + 1) * CH], b if right else TW - b, 1)
        keep = lane >= b if right else lane < TW - b
        total = total + jnp.where(keep, part, 0.0)
    return total


def lanes():
    return lax.broadcasted_iota(jnp.int32, (CH, TW), 1)


def shrunk(moved, cut):
    return moved - jnp.clip(moved, -cut, cut)


def synthesize(w, sources, first, mine_ref, theirs_ref):
    lane = lanes()
    for i, q in enumerate(products(w, sources, first, EXT)):
        s = gathered(q, lane, True)
        mine_ref[i] = s[:HALF]
        theirs_ref[i] = s[HALF:]


def first_kernel(sets, *refs):
    main, above, ws = refs[:sets], refs[sets : 2 * sets], refs[2 * sets : 3 * sets]
    mine_ref, theirs_ref = refs[3 * sets : 3 * sets + 2]
    his, los = refs[3 * sets + 2 : 4 * sets + 2], refs[4 * sets + 2 :]
    for s in range(sets):
        for r in range(ROWS):
            his[s][r], los[s][r] = split(above[s][pl.ds(r, CH, stride=ROWS), :])
            his[s][ROWS + r], los[s][ROWS + r] = split(main[s][pl.ds(r, CH, stride=ROWS), :])
    synthesize(weights(ws, 1), his + los, ROWS - 2 * RIM, mine_ref, theirs_ref)


def load_misfit(mine_ref, theirs_ref, hi_ref, lo_ref, count):
    for r in range(count):
        hi_ref[r], lo_ref[r] = split(jnp.concatenate([mine_ref[r], theirs_ref[r]], axis=0))


def second_kernel(sets, tile_ref, m_ref, t_ref, *refs):
    groups = [refs[n * sets : (n + 1) * sets] for n in range(6)]
    main, above, below, cuts, wrs, wss = groups
    z1_ref, mine_ref, theirs_ref, mhi_ref, mlo_ref = refs[6 * sets : 6 * sets + 5]
    his, los = refs[6 * sets + 5 : 7 * sets + 5], refs[7 * sets + 5 :]
    load_misfit(m_ref, t_ref, mhi_ref, mlo_ref, ROWS + 3 * RIM)
    lane = lanes()
    tile = tile_ref[0]
    for n, q in enumerate(products(weights(wrs, 0), [mhi_ref, mlo_ref], 0, ROWS + 2 * RIM)):
        i = n - RIM
        for s in range(sets):
            r = gathered(q[s * TAPS : (s + 1) * TAPS], lane, False)
            if i < 0:
                z = above[s][pl.ds(i + ROWS, CH, stride=ROWS), :]
            elif i < ROWS:
                z = main[s][pl.ds(i, CH, stride=ROWS), :]
            else:
                z = below[s][i - ROWS]
            z = shrunk(z - STEP * r, cuts[s][...])
            if i < 0:
                z = jnp.where(tile > 0, z, 0.0)
            elif i >= ROWS:
                z = jnp.where(tile < tile_ref[1], z, 0.0)
            elif s == 0:
                z1_ref[i] = z
            his[s][n], los[s][n] = split(z)
    synthesize(weights(wss, 1), his + los, 0, mine_ref, theirs_ref)


def third_kernel(
    tile_ref, z_ref, m_ref, t_ref, cut_ref, wr_ref, coded_ref, misfit_ref, hi_ref, lo_ref
):
    lane = lanes()
    cut = cut_ref[...]
    own = tile_ref[2] == 0
    last = tile_ref[0] == tile_ref[1]
    for i in range(EXT):
        m, t = m_ref[i], t_ref[i]
        both = jnp.concatenate([m, t], axis=0)
        if i >= ROWS:
            both = jnp.where(last, 0.0, both)
        else:
            misfit_ref[pl.ds(i, HALF, stride=ROWS), :] = jnp.where(own, m, t)
            misfit_ref[pl.ds(HALF * ROWS + i, HALF, stride=ROWS), :] = jnp.where(own, t, m)
        hi_ref[i], lo_ref[i] = split(both)
    for i, q in enumerate(products(weights([wr_ref], 0), [hi_ref, lo_ref], 0, ROWS)):
        z = shrunk(z_ref[i] - STEP * gathered(q, lane, False), cut)
        coded_ref[pl.ds(i, CH, stride=ROWS), :] = z


VMEM = pl.BlockSpec(memory_space=pltpu.VMEM)
SMEM = pl.BlockSpec(memory_space=pltpu.SMEM)


def f32(*shape):
    return jax.ShapeDtypeStruct(shape, jnp.float32)


def bf16(rows):
    return pltpu.VMEM((rows, CH, TW), jnp.bfloat16)


def call(kernel, in_specs, outs, scratch, flops):
    return pl.pallas_call(
        kernel,
        in_specs=in_specs,
        out_specs=[VMEM] * len(outs),
        out_shape=outs,
        scratch_shapes=scratch,
        compiler_params=pltpu.CompilerParams(vmem_limit_bytes=16 << 20),
        cost_estimate=pl.CostEstimate(
            flops=flops, bytes_accessed=1 << 20, transcendentals=0
        ),
    )


def send(x, by=0, mask=0):
    tiles, atoms = lax.axis_size("tile"), lax.axis_size("atom")
    if by == 0:
        return lax.ppermute(x, "atom", [(i, i ^ mask) for i in range(atoms)])
    if mask == 0:
        return lax.ppermute(
            x, "tile", [(t, t + by) for t in range(tiles) if 0 <= t + by < tiles]
        )
    pairs = [
        (t * atoms + i, (t + by) * atoms + (i ^ mask))
        for t in range(tiles)
        if 0 <= t + by < tiles
        for i in range(atoms)
    ]
    return lax.ppermute(x, ("tile", "atom"), pairs)


def summed(mine, theirs):
    total = mine + send(theirs, mask=1)
    for mask in BUTTERFLY:
        total = total + send(total, mask=mask)
    return total


def per_device(observed, coefficients, dictionary, thresholds):
    core = lax.axis_index("atom") % 2
    tile = lax.axis_index("tile")
    place = jnp.stack([tile, jnp.full_like(tile, lax.axis_size("tile") - 1), core]).astype(jnp.int32)
    z0 = coefficients.reshape(CH * ROWS, TW)
    main = [z0]
    if PARTNER:
        main.append(send(z0, mask=PARTNER))
    obs = jnp.transpose(
        jnp.where(core == 0, observed[:HALF], observed[HALF:]), (1, 0, 2)
    )
    rolled = jnp.where(
        core == 0,
        dictionary,
        jnp.concatenate([dictionary[:, HALF:], dictionary[:, :HALF]], axis=1),
    )
    ws = [jnp.transpose(rolled[:, :, ::-1, :], (3, 1, 2, 0)).reshape(TAPS, TAPS)]
    wr = [jnp.transpose(rolled, (3, 0, 2, 1)).reshape(TAPS, TAPS)]
    cut = [jnp.broadcast_to((STEP * thresholds)[:, None], (CH, TW))]
    own = jnp.concatenate([ws[0], wr[0], cut[0]], axis=0)
    down = main + [obs[ROWS - RIM :].reshape(RIM * HALF, TW)]
    if PARTNER:
        main[1], own = lax.optimization_barrier((main[1], own))
        down[1] = main[1]
    from_above = send(jnp.concatenate(down, axis=0), by=1)
    above = [from_above[s * CH * ROWS : (s + 1) * CH * ROWS] for s in range(len(main))]
    obs_above = from_above[len(main) * CH * ROWS :].reshape(RIM, HALF, TW)
    if PARTNER:
        theirs = send(own, mask=PARTNER)
        ws.append(theirs[:TAPS])
        wr.append(theirs[TAPS : 2 * TAPS])
        cut.append(theirs[2 * TAPS :])
    sets = len(main)
    part = f32(EXT, HALF, TW)

    mine, theirs = call(
        lambda *refs: first_kernel(sets, *refs),
        [VMEM] * (3 * sets),
        [part, part],
        [bf16(2 * ROWS)] * (2 * sets),
        sets << 29,
    )(*main, *above, *ws)
    misfit = summed(mine, theirs) - jnp.concatenate([obs_above, obs], axis=0)

    rows0 = [
        jnp.transpose(z.reshape(CH, ROWS, TW)[:, :RIM], (1, 0, 2)).reshape(RIM * CH, TW)
        for z in main
    ]
    up = jnp.concatenate(
        [
            misfit[RIM : 3 * RIM].reshape(2 * RIM * HALF, TW),
            obs[:RIM].reshape(RIM * HALF, TW),
            *rows0,
        ],
        axis=0,
    )
    from_below = send(up, by=-1)
    cuts_at = [2 * RIM * HALF, 3 * RIM * HALF]
    obs_below = from_below[cuts_at[0] : cuts_at[1]].reshape(RIM, HALF, TW)
    below = [
        from_below[cuts_at[1] + s * RIM * CH : cuts_at[1] + (s + 1) * RIM * CH].reshape(RIM, CH, TW)
        for s in range(sets)
    ]
    m = jnp.concatenate(
        [misfit, from_below[: cuts_at[0]].reshape(2 * RIM, HALF, TW)], axis=0
    )
    t = send(m, mask=1)
    z1, mine, theirs = call(
        lambda *refs: second_kernel(sets, *refs),
        [SMEM] + [VMEM] * (2 + 6 * sets),
        [f32(ROWS, CH, TW), part, part],
        [bf16(ROWS + 3 * RIM)] * 2 + [bf16(ROWS + 2 * RIM)] * (2 * sets),
        sets << 30,
    )(place, m, t, *main, *above, *below, *cut, *wr, *ws)
    m = summed(mine, theirs) - jnp.concatenate([obs, obs_below], axis=0)
    t = send(m, mask=1)
    coded, out = call(
        third_kernel,
        [SMEM] + [VMEM] * 5,
        [f32(CH * ROWS, TW), f32(CH * ROWS, TW)],
        [bf16(EXT)] * 2,
        1 << 29,
    )(place, z1, m, t, cut[0], wr[0])
    return coded.reshape(CH, ROWS, TW), out.reshape(CH, ROWS, TW)


def solution(mesh):
    in_specs = (
        P(None, "tile", None),
        P("atom", "tile", None),
        P("atom", None, None, None),
        P("atom"),
    )
    out_specs = (P("atom", "tile", None), P(None, "tile", None))
    return jax.shard_map(
        per_device, mesh=mesh, in_specs=in_specs, out_specs=out_specs, check_vma=False
    )
```

```python
import jax
import jax.numpy as jnp
from jax import lax
from jax.experimental import pallas as pl
from jax.experimental.pallas import tpu as pltpu
from jax.sharding import PartitionSpec as P

STEP = 8.0
KS = 8
RIM = KS - 1
ROWS = 16
CH = 16
HALF = CH // 2
TW = 128
TAPS = KS * CH
EXT = ROWS + RIM
BUTTERFLY = (2, 4, 8, 24)


def split(x):
    hi = x.astype(jnp.bfloat16)
    lo = (x - hi.astype(jnp.float32)).astype(jnp.bfloat16)
    return hi, lo


def stacked(hi, lo):
    return jnp.concatenate(
        [jnp.concatenate([hi, hi], axis=1), jnp.concatenate([lo, lo], axis=1)], axis=0
    )


def weights(ref):
    return stacked(*split(ref[...]))


def products(w, sources, first, count):
    out = []
    half = w.shape[0] // 2
    for i in range(0, count, 2):
        pair = min(2, count - i)
        window = [
            jnp.concatenate(
                [
                    ref[first + i + d : first + i + d + KS].reshape(TAPS, TW)
                    for ref in sources
                ],
                axis=0,
            )
            for d in range(pair)
        ]
        x = jnp.concatenate(window, axis=1) if pair == 2 else window[0]
        q = jnp.dot(w, x, preferred_element_type=jnp.float32)
        q = q[:half] + q[half:]
        for d in range(pair):
            out.append(q[:, d * TW : (d + 1) * TW])
    return out


def gathered(q, lane, right):
    total = q[:CH]
    for b in range(1, KS):
        part = pltpu.roll(q[b * CH : (b + 1) * CH], b if right else TW - b, 1)
        keep = lane >= b if right else lane < TW - b
        total = total + jnp.where(keep, part, 0.0)
    return total


def lanes():
    return lax.broadcasted_iota(jnp.int32, (CH, TW), 1)


def shrunk(moved, cut):
    return moved - jnp.clip(moved, -cut, cut)


def synthesize(w, sources, own, mine_ref, theirs_ref):
    lane = lanes()
    for i, q in enumerate(products(w, sources, 0, EXT)):
        s = gathered(q, lane, True)
        mine_ref[i] = jnp.where(own, s[:HALF], s[HALF:])
        theirs_ref[i] = jnp.where(own, s[HALF:], s[:HALF])


def first_kernel(place_ref, z_ref, ws_ref, mine_ref, theirs_ref, hi_ref, lo_ref):
    zero = jnp.zeros((CH, TW), jnp.bfloat16)
    for r in range(ROWS + 2 * RIM):
        if RIM <= r < EXT:
            hi_ref[r], lo_ref[r] = split(z_ref[pl.ds(r - RIM, CH, stride=ROWS), :])
        else:
            hi_ref[r] = zero
            lo_ref[r] = zero
    synthesize(weights(ws_ref), [hi_ref, lo_ref], place_ref[2] == 0, mine_ref, theirs_ref)


def bands(own, m, t):
    return jnp.where(own, jnp.concatenate([m, t], axis=0), jnp.concatenate([t, m], axis=0))


def second_kernel(
    place_ref, m_ref, t_ref, z_ref, above_ref, below_ref, cut_ref, wr_ref, ws_ref,
    z1_ref, mine_ref, theirs_ref, mhi_ref, mlo_ref, hi_ref, lo_ref,
):
    tile, last = place_ref[0], place_ref[1]
    own = place_ref[2] == 0
    for r in range(ROWS + 3 * RIM):
        mhi_ref[r], mlo_ref[r] = split(bands(own, m_ref[r], t_ref[r]))
    lane = lanes()
    cut = cut_ref[...]
    for n, q in enumerate(products(weights(wr_ref), [mhi_ref, mlo_ref], 0, ROWS + 2 * RIM)):
        i = n - RIM
        if i < 0:
            z = above_ref[n]
        elif i < ROWS:
            z = z_ref[pl.ds(i, CH, stride=ROWS), :]
        else:
            z = below_ref[i - ROWS]
        z = shrunk(z - STEP * gathered(q, lane, False), cut)
        if i < 0:
            z = jnp.where(tile > 0, z, 0.0)
        elif i >= ROWS:
            z = jnp.where(tile < last, z, 0.0)
        else:
            z1_ref[i] = z
        hi_ref[n], lo_ref[n] = split(z)
    synthesize(weights(ws_ref), [hi_ref, lo_ref], own, mine_ref, theirs_ref)


def third_kernel(
    place_ref, z_ref, m_ref, t_ref, cut_ref, wr_ref, coded_ref, misfit_ref, hi_ref, lo_ref
):
    lane = lanes()
    cut = cut_ref[...]
    own = place_ref[2] == 0
    inside = place_ref[0] < place_ref[1]
    for i in range(EXT):
        both = bands(own, m_ref[i], t_ref[i])
        if i < ROWS:
            misfit_ref[pl.ds(i, CH, stride=ROWS), :] = both
        else:
            both = jnp.where(inside, both, 0.0)
        hi_ref[i], lo_ref[i] = split(both)
    for i, q in enumerate(products(weights(wr_ref), [hi_ref, lo_ref], 0, ROWS)):
        z = shrunk(z_ref[i] - STEP * gathered(q, lane, False), cut)
        coded_ref[pl.ds(i, CH, stride=ROWS), :] = z


VMEM = pl.BlockSpec(memory_space=pltpu.VMEM)
SMEM = pl.BlockSpec(memory_space=pltpu.SMEM)


def f32(*shape):
    return jax.ShapeDtypeStruct(shape, jnp.float32)


def bf16(rows):
    return pltpu.VMEM((rows, CH, TW), jnp.bfloat16)


def call(kernel, in_specs, outs, scratch, flops):
    return pl.pallas_call(
        kernel,
        in_specs=in_specs,
        out_specs=[VMEM] * len(outs),
        out_shape=outs,
        scratch_shapes=scratch,
        compiler_params=pltpu.CompilerParams(vmem_limit_bytes=16 << 20),
        cost_estimate=pl.CostEstimate(
            flops=flops, bytes_accessed=1 << 20, transcendentals=0
        ),
    )


def across(x, mask):
    n = lax.axis_size("atom")
    return lax.ppermute(x, "atom", [(i, i ^ mask) for i in range(n)])


def shifted(x, by):
    n = lax.axis_size("tile")
    return lax.ppermute(x, "tile", [(t, t + by) for t in range(n) if 0 <= t + by < n])


def summed(mine, theirs):
    total = mine + across(theirs, 1)
    for mask in BUTTERFLY:
        total = total + across(total, mask)
    return total


def flat(x):
    return x.reshape(-1, TW)


def per_device(observed, coefficients, dictionary, thresholds):
    core = lax.axis_index("atom") % 2
    tile = lax.axis_index("tile")
    last = lax.axis_size("tile") - 1
    place = jnp.stack([tile, jnp.full_like(tile, last), core]).astype(jnp.int32)
    z0 = flat(coefficients)
    ws = jnp.transpose(dictionary[:, :, ::-1, :], (3, 1, 2, 0)).reshape(TAPS, TAPS)
    wr = jnp.transpose(dictionary, (3, 0, 2, 1)).reshape(TAPS, TAPS)
    cut = jnp.broadcast_to((STEP * thresholds)[:, None], (CH, TW))
    obs = jnp.transpose(
        jnp.where(core == 0, observed[:HALF], observed[HALF:]), (1, 0, 2)
    )
    part = f32(EXT, HALF, TW)

    mine, theirs = call(
        first_kernel,
        [SMEM, VMEM, VMEM],
        [part, part],
        [bf16(ROWS + 2 * RIM)] * 2,
        1 << 29,
    )(place, z0, ws)
    total = summed(mine, theirs)
    inner = total[:ROWS] - obs
    outer = total[ROWS:]
    top = jnp.transpose(coefficients[:, :RIM], (1, 0, 2))
    bottom = jnp.transpose(coefficients[:, ROWS - RIM :], (1, 0, 2))
    down = shifted(
        jnp.concatenate([flat(inner[ROWS - RIM :]), flat(outer), flat(bottom)], axis=0), 1
    )
    up = shifted(
        jnp.concatenate([flat(inner[: 2 * RIM]), flat(obs[:RIM]), flat(top)], axis=0), -1
    )
    side = RIM * HALF
    above_misfit = down[:side].reshape(RIM, HALF, TW)
    above_adds = down[side : 2 * side].reshape(RIM, HALF, TW)
    above = down[2 * side :].reshape(RIM, CH, TW)
    below_misfit = up[: 2 * side].reshape(2 * RIM, HALF, TW)
    obs_below = up[2 * side : 3 * side].reshape(RIM, HALF, TW)
    below = up[3 * side :].reshape(RIM, CH, TW)
    m = jnp.concatenate(
        [
            above_misfit,
            inner[:RIM] + above_adds,
            inner[RIM:],
            jnp.where(tile < last, below_misfit[:RIM] + outer, 0.0),
            below_misfit[RIM:],
        ],
        axis=0,
    )
    t = across(m, 1)
    z1, mine, theirs = call(
        second_kernel,
        [SMEM] + [VMEM] * 8,
        [f32(ROWS, CH, TW), part, part],
        [bf16(ROWS + 3 * RIM)] * 2 + [bf16(ROWS + 2 * RIM)] * 2,
        1 << 30,
    )(place, m, t, z0, above, below, cut, wr, ws)
    m = summed(mine, theirs) - jnp.concatenate([obs, obs_below], axis=0)
    t = across(m, 1)
    coded, out = call(
        third_kernel,
        [SMEM] + [VMEM] * 5,
        [f32(CH * ROWS, TW), f32(CH * ROWS, TW)],
        [bf16(EXT)] * 2,
        1 << 29,
    )(place, z1, m, t, cut, wr)
    return coded.reshape(CH, ROWS, TW), out.reshape(CH, ROWS, TW)


def solution(mesh):
    in_specs = (
        P(None, "tile", None),
        P("atom", "tile", None),
        P("atom", None, None, None),
        P("atom"),
    )
    out_specs = (P("atom", "tile", None), P(None, "tile", None))
    return jax.shard_map(
        per_device, mesh=mesh, in_specs=in_specs, out_specs=out_specs, check_vma=False
    )
```

```python
import jax
import jax.numpy as jnp
from jax import lax
from jax.experimental import pallas as pl
from jax.experimental.pallas import tpu as pltpu
from jax.sharding import PartitionSpec as P

STEP = 8.0
KS = 8
RIM = KS - 1
ROWS = 16
CH = 16
HALF = CH // 2
TW = 128
TAPS = KS * CH
EXT = ROWS + RIM
BUTTERFLY = (2, 4, 8, 24)


def split(x):
    hi = x.astype(jnp.bfloat16)
    lo = (x - hi.astype(jnp.float32)).astype(jnp.bfloat16)
    return hi, lo


def stacked(hi, lo):
    return jnp.concatenate(
        [jnp.concatenate([hi, hi], axis=1), jnp.concatenate([lo, lo], axis=1)], axis=0
    )


def weights(ref, turned=False):
    w = ref[...]
    return stacked(*split(w.T if turned else w))


def products(w, sources, count, backwards=False):
    half = w.shape[0] // 2
    for i in range(0, count, 2):
        pair = min(2, count - i)
        window = [
            jnp.concatenate(
                [
                    ref[i + d + RIM - a] if backwards else ref[i + d + a]
                    for ref in sources
                    for a in range(KS)
                ],
                axis=0,
            )
            for d in range(pair)
        ]
        x = jnp.concatenate(window, axis=1) if pair == 2 else window[0]
        q = jnp.dot(w, x, preferred_element_type=jnp.float32)
        q = q[:half] + q[half:]
        for d in range(pair):
            yield q[:, d * TW : (d + 1) * TW]


def gathered(q, lane, right):
    total = q[:CH]
    for b in range(1, KS):
        part = pltpu.roll(q[b * CH : (b + 1) * CH], b if right else TW - b, 1)
        keep = lane >= b if right else lane < TW - b
        total = total + jnp.where(keep, part, 0.0)
    return total


def lanes():
    return lax.broadcasted_iota(jnp.int32, (CH, TW), 1)


def shrunk(moved, cut):
    return moved - jnp.clip(moved, -cut, cut)


def synthesize(w, sources, own, mine_ref, theirs_ref):
    lane = lanes()
    for i, q in enumerate(products(w, sources, EXT, True)):
        s = gathered(q, lane, True)
        mine_ref[i] = jnp.where(own, s[:HALF], s[HALF:])
        theirs_ref[i] = jnp.where(own, s[HALF:], s[:HALF])


def first_kernel(place_ref, z_ref, ws_ref, mine_ref, theirs_ref, hi_ref, lo_ref):
    zero = jnp.zeros((CH, TW), jnp.bfloat16)
    for r in range(ROWS + 2 * RIM):
        if RIM <= r < EXT:
            hi_ref[r], lo_ref[r] = split(z_ref[pl.ds(r - RIM, CH, stride=ROWS), :])
        else:
            hi_ref[r] = zero
            lo_ref[r] = zero
    synthesize(weights(ws_ref, True), [hi_ref, lo_ref], place_ref[2] == 0, mine_ref, theirs_ref)


def bands(own, m, t):
    return jnp.where(own, jnp.concatenate([m, t], axis=0), jnp.concatenate([t, m], axis=0))


def second_kernel(
    place_ref, m_ref, t_ref, z_ref, above_ref, below_ref, cut_ref, wr_ref, ws_ref,
    z1_ref, mine_ref, theirs_ref, mhi_ref, mlo_ref, hi_ref, lo_ref,
):
    tile, last = place_ref[0], place_ref[1]
    own = place_ref[2] == 0
    for r in range(ROWS + 3 * RIM):
        mhi_ref[r], mlo_ref[r] = split(bands(own, m_ref[r], t_ref[r]))
    lane = lanes()
    cut = cut_ref[...]
    for n, q in enumerate(products(weights(wr_ref), [mhi_ref, mlo_ref], ROWS + 2 * RIM)):
        i = n - RIM
        if i < 0:
            z = above_ref[n]
        elif i < ROWS:
            z = z_ref[pl.ds(i, CH, stride=ROWS), :]
        else:
            z = below_ref[i - ROWS]
        z = shrunk(z - STEP * gathered(q, lane, False), cut)
        if i < 0:
            z = jnp.where(tile > 0, z, 0.0)
        elif i >= ROWS:
            z = jnp.where(tile < last, z, 0.0)
        else:
            z1_ref[i] = z
        hi_ref[n], lo_ref[n] = split(z)
    synthesize(weights(ws_ref, True), [hi_ref, lo_ref], own, mine_ref, theirs_ref)


def third_kernel(
    place_ref, z_ref, m_ref, t_ref, cut_ref, wr_ref, coded_ref, misfit_ref, hi_ref, lo_ref
):
    lane = lanes()
    cut = cut_ref[...]
    own = place_ref[2] == 0
    inside = place_ref[0] < place_ref[1]
    for i in range(EXT):
        both = bands(own, m_ref[i], t_ref[i])
        if i < ROWS:
            misfit_ref[pl.ds(i, CH, stride=ROWS), :] = both
        else:
            both = jnp.where(inside, both, 0.0)
        hi_ref[i], lo_ref[i] = split(both)
    for i, q in enumerate(products(weights(wr_ref), [hi_ref, lo_ref], ROWS)):
        z = shrunk(z_ref[i] - STEP * gathered(q, lane, False), cut)
        coded_ref[pl.ds(i, CH, stride=ROWS), :] = z


VMEM = pl.BlockSpec(memory_space=pltpu.VMEM)
SMEM = pl.BlockSpec(memory_space=pltpu.SMEM)


def f32(*shape):
    return jax.ShapeDtypeStruct(shape, jnp.float32)


def bf16(rows):
    return pltpu.VMEM((rows, CH, TW), jnp.bfloat16)


def call(kernel, in_specs, outs, scratch, flops):
    return pl.pallas_call(
        kernel,
        in_specs=in_specs,
        out_specs=[VMEM] * len(outs),
        out_shape=outs,
        scratch_shapes=scratch,
        compiler_params=pltpu.CompilerParams(vmem_limit_bytes=16 << 20),
        cost_estimate=pl.CostEstimate(
            flops=flops, bytes_accessed=1 << 20, transcendentals=0
        ),
    )


def across(x, mask):
    n = lax.axis_size("atom")
    return lax.ppermute(x, "atom", [(i, i ^ mask) for i in range(n)])


def shifted(x, by):
    n = lax.axis_size("tile")
    return lax.ppermute(x, "tile", [(t, t + by) for t in range(n) if 0 <= t + by < n])


def summed(mine, theirs):
    total = mine + across(theirs, 1)
    for mask in BUTTERFLY:
        total = total + across(total, mask)
    return total


def flat(x):
    return x.reshape(-1, TW)


def per_device(observed, coefficients, dictionary, thresholds):
    core = lax.axis_index("atom") % 2
    tile = lax.axis_index("tile")
    last = lax.axis_size("tile") - 1
    place = jnp.stack([tile, jnp.full_like(tile, last), core]).astype(jnp.int32)
    z0 = flat(coefficients)
    ws = jnp.transpose(dictionary, (2, 0, 3, 1)).reshape(TAPS, TAPS)
    wr = jnp.transpose(dictionary, (3, 0, 2, 1)).reshape(TAPS, TAPS)
    cut = jnp.broadcast_to((STEP * thresholds)[:, None], (CH, TW))
    obs = jnp.transpose(
        jnp.where(core == 0, observed[:HALF], observed[HALF:]), (1, 0, 2)
    )
    part = f32(EXT, HALF, TW)

    mine, theirs = call(
        first_kernel,
        [SMEM, VMEM, VMEM],
        [part, part],
        [bf16(ROWS + 2 * RIM)] * 2,
        1 << 29,
    )(place, z0, ws)
    total = summed(mine, theirs)
    inner = total[:ROWS] - obs
    outer = total[ROWS:]
    top = jnp.transpose(coefficients[:, :RIM], (1, 0, 2))
    bottom = jnp.transpose(coefficients[:, ROWS - RIM :], (1, 0, 2))
    up = shifted(
        jnp.concatenate([flat(inner[: 2 * RIM]), flat(obs[:RIM]), flat(top)], axis=0), -1
    )
    down = shifted(
        jnp.concatenate([flat(inner[ROWS - RIM :]), flat(outer), flat(bottom)], axis=0), 1
    )
    side = RIM * HALF
    above_misfit = down[:side].reshape(RIM, HALF, TW)
    above_adds = down[side : 2 * side].reshape(RIM, HALF, TW)
    above = down[2 * side :].reshape(RIM, CH, TW)
    below_misfit = up[: 2 * side].reshape(2 * RIM, HALF, TW)
    obs_below = up[2 * side : 3 * side].reshape(RIM, HALF, TW)
    below = up[3 * side :].reshape(RIM, CH, TW)
    m = jnp.concatenate(
        [
            above_misfit,
            inner[:RIM] + above_adds,
            inner[RIM:],
            jnp.where(tile < last, below_misfit[:RIM] + outer, 0.0),
            below_misfit[RIM:],
        ],
        axis=0,
    )
    t = across(m, 1)
    z1, mine, theirs = call(
        second_kernel,
        [SMEM] + [VMEM] * 8,
        [f32(ROWS, CH, TW), part, part],
        [bf16(ROWS + 3 * RIM)] * 2 + [bf16(ROWS + 2 * RIM)] * 2,
        1 << 30,
    )(place, m, t, z0, above, below, cut, wr, ws)
    m = summed(mine, theirs) - jnp.concatenate([obs, obs_below], axis=0)
    t = across(m, 1)
    coded, out = call(
        third_kernel,
        [SMEM] + [VMEM] * 5,
        [f32(CH * ROWS, TW), f32(CH * ROWS, TW)],
        [bf16(EXT)] * 2,
        1 << 29,
    )(place, z1, m, t, cut, wr)
    return coded.reshape(CH, ROWS, TW), out.reshape(CH, ROWS, TW)


def solution(mesh):
    in_specs = (
        P(None, "tile", None),
        P("atom", "tile", None),
        P("atom", None, None, None),
        P("atom"),
    )
    out_specs = (P("atom", "tile", None), P(None, "tile", None))
    return jax.shard_map(
        per_device, mesh=mesh, in_specs=in_specs, out_specs=out_specs, check_vma=False
    )
```

```python
import jax
import jax.numpy as jnp
from jax import lax
from jax.experimental import pallas as pl
from jax.experimental.pallas import tpu as pltpu
from jax.sharding import PartitionSpec as P

STEP = 8.0
KS = 8
RIM = KS - 1
ROWS = 16
CH = 16
HALF = CH // 2
TW = 128
TAPS = KS * CH
EXT = ROWS + RIM
BUTTERFLY = (2, 4, 8, 24)


def split(x):
    hi = x.astype(jnp.bfloat16)
    lo = (x - hi.astype(jnp.float32)).astype(jnp.bfloat16)
    return hi, lo


def stacked(hi, lo):
    return jnp.concatenate(
        [jnp.concatenate([hi, hi], axis=1), jnp.concatenate([lo, lo], axis=1)], axis=0
    )


def weights(ref, turned=False):
    w = ref[...]
    return stacked(*split(w.T if turned else w))


def products(w, sources, count, backwards=False):
    half = w.shape[0] // 2
    for i in range(0, count, 2):
        pair = min(2, count - i)
        window = [
            jnp.concatenate(
                [
                    ref[i + d + RIM - a] if backwards else ref[i + d + a]
                    for ref in sources
                    for a in range(KS)
                ],
                axis=0,
            )
            for d in range(pair)
        ]
        x = jnp.concatenate(window, axis=1) if pair == 2 else window[0]
        q = jnp.dot(w, x, preferred_element_type=jnp.float32)
        q = q[:half] + q[half:]
        for d in range(pair):
            yield q[:, d * TW : (d + 1) * TW]


def gathered(q, lane, right):
    total = q[:CH]
    for b in range(1, KS):
        part = pltpu.roll(q[b * CH : (b + 1) * CH], b if right else TW - b, 1)
        keep = lane >= b if right else lane < TW - b
        total = total + jnp.where(keep, part, 0.0)
    return total


def lanes():
    return lax.broadcasted_iota(jnp.int32, (CH, TW), 1)


def shrunk(moved, cut):
    return moved - jnp.clip(moved, -cut, cut)


def synthesize(w, sources, own, mine_ref, theirs_ref):
    lane = lanes()
    for i, q in enumerate(products(w, sources, EXT, True)):
        s = gathered(q, lane, True)
        mine_ref[i] = jnp.where(own, s[:HALF], s[HALF:])
        theirs_ref[i] = jnp.where(own, s[HALF:], s[:HALF])


def first_kernel(place_ref, z_ref, ws_ref, mine_ref, theirs_ref, hi_ref, lo_ref):
    zero = jnp.zeros((CH, TW), jnp.bfloat16)
    for r in range(ROWS + 2 * RIM):
        if RIM <= r < EXT:
            hi_ref[r], lo_ref[r] = split(z_ref[pl.ds(r - RIM, CH, stride=ROWS), :])
        else:
            hi_ref[r] = zero
            lo_ref[r] = zero
    synthesize(weights(ws_ref, True), [hi_ref, lo_ref], place_ref[2] == 0, mine_ref, theirs_ref)


def bands(own, m, t):
    return jnp.where(own, jnp.concatenate([m, t], axis=0), jnp.concatenate([t, m], axis=0))


def second_kernel(
    place_ref, m_ref, t_ref, z_ref, above_ref, below_ref, cut_ref, wr_ref, ws_ref,
    z1_ref, mine_ref, theirs_ref, mhi_ref, mlo_ref, hi_ref, lo_ref,
):
    tile, last = place_ref[0], place_ref[1]
    own = place_ref[2] == 0
    for r in range(ROWS + 3 * RIM):
        mhi_ref[r], mlo_ref[r] = split(bands(own, m_ref[r], t_ref[r]))
    lane = lanes()
    cut = cut_ref[...]
    for n, q in enumerate(products(weights(wr_ref), [mhi_ref, mlo_ref], ROWS + 2 * RIM)):
        i = n - RIM
        if i < 0:
            z = above_ref[n]
        elif i < ROWS:
            z = z_ref[pl.ds(i, CH, stride=ROWS), :]
        else:
            z = below_ref[i - ROWS]
        stepped = shrunk(z - STEP * gathered(q, lane, False), cut)
        change = stepped - z
        if i < 0:
            change = jnp.where(tile > 0, change, 0.0)
        elif i >= ROWS:
            change = jnp.where(tile < last, change, 0.0)
        else:
            z1_ref[i] = stepped
        hi_ref[n], lo_ref[n] = split(change)
    synthesize(weights(ws_ref, True), [hi_ref, lo_ref], own, mine_ref, theirs_ref)


def third_kernel(
    place_ref, z_ref, m_ref, t_ref, cut_ref, wr_ref, coded_ref, misfit_ref, hi_ref, lo_ref
):
    lane = lanes()
    cut = cut_ref[...]
    own = place_ref[2] == 0
    inside = place_ref[0] < place_ref[1]
    for i in range(EXT):
        both = bands(own, m_ref[i], t_ref[i])
        if i < ROWS:
            misfit_ref[pl.ds(i, CH, stride=ROWS), :] = both
        else:
            both = jnp.where(inside, both, 0.0)
        hi_ref[i], lo_ref[i] = split(both)
    for i, q in enumerate(products(weights(wr_ref), [hi_ref, lo_ref], ROWS)):
        z = shrunk(z_ref[i] - STEP * gathered(q, lane, False), cut)
        coded_ref[pl.ds(i, CH, stride=ROWS), :] = z


VMEM = pl.BlockSpec(memory_space=pltpu.VMEM)
SMEM = pl.BlockSpec(memory_space=pltpu.SMEM)


def f32(*shape):
    return jax.ShapeDtypeStruct(shape, jnp.float32)


def bf16(rows):
    return pltpu.VMEM((rows, CH, TW), jnp.bfloat16)


def call(kernel, in_specs, outs, scratch, flops):
    return pl.pallas_call(
        kernel,
        in_specs=in_specs,
        out_specs=[VMEM] * len(outs),
        out_shape=outs,
        scratch_shapes=scratch,
        compiler_params=pltpu.CompilerParams(vmem_limit_bytes=16 << 20),
        cost_estimate=pl.CostEstimate(
            flops=flops, bytes_accessed=1 << 20, transcendentals=0
        ),
    )


def across(x, mask):
    n = lax.axis_size("atom")
    return lax.ppermute(x, "atom", [(i, i ^ mask) for i in range(n)])


def shifted(x, by):
    n = lax.axis_size("tile")
    return lax.ppermute(x, "tile", [(t, t + by) for t in range(n) if 0 <= t + by < n])


def summed(mine, theirs):
    total = mine + across(theirs, 1)
    for mask in BUTTERFLY:
        total = total + across(total, mask)
    return total


def flat(x):
    return x.reshape(-1, TW)


def per_device(observed, coefficients, dictionary, thresholds):
    core = lax.axis_index("atom") % 2
    tile = lax.axis_index("tile")
    last = lax.axis_size("tile") - 1
    place = jnp.stack([tile, jnp.full_like(tile, last), core]).astype(jnp.int32)
    z0 = flat(coefficients)
    ws = jnp.transpose(dictionary, (2, 0, 3, 1)).reshape(TAPS, TAPS)
    wr = jnp.transpose(dictionary, (3, 0, 2, 1)).reshape(TAPS, TAPS)
    cut = jnp.broadcast_to((STEP * thresholds)[:, None], (CH, TW))
    obs = jnp.transpose(
        jnp.where(core == 0, observed[:HALF], observed[HALF:]), (1, 0, 2)
    )
    part = f32(EXT, HALF, TW)

    mine, theirs = call(
        first_kernel,
        [SMEM, VMEM, VMEM],
        [part, part],
        [bf16(ROWS + 2 * RIM)] * 2,
        1 << 29,
    )(place, z0, ws)
    total = summed(mine, theirs)
    inner = total[:ROWS] - obs
    outer = total[ROWS:]
    top = jnp.transpose(coefficients[:, :RIM], (1, 0, 2))
    bottom = jnp.transpose(coefficients[:, ROWS - RIM :], (1, 0, 2))
    up = shifted(
        jnp.concatenate([flat(inner[: 2 * RIM]), flat(top)], axis=0), -1
    )
    down = shifted(
        jnp.concatenate([flat(inner[ROWS - RIM :]), flat(outer), flat(bottom)], axis=0), 1
    )
    side = RIM * HALF
    above_misfit = down[:side].reshape(RIM, HALF, TW)
    above_adds = down[side : 2 * side].reshape(RIM, HALF, TW)
    above = down[2 * side :].reshape(RIM, CH, TW)
    below_misfit = up[: 2 * side].reshape(2 * RIM, HALF, TW)
    below = up[2 * side :].reshape(RIM, CH, TW)
    m = jnp.concatenate(
        [
            above_misfit,
            inner[:RIM] + above_adds,
            inner[RIM:],
            jnp.where(tile < last, below_misfit[:RIM] + outer, 0.0),
            below_misfit[RIM:],
        ],
        axis=0,
    )
    t = across(m, 1)
    z1, mine, theirs = call(
        second_kernel,
        [SMEM] + [VMEM] * 8,
        [f32(ROWS, CH, TW), part, part],
        [bf16(ROWS + 3 * RIM)] * 2 + [bf16(ROWS + 2 * RIM)] * 2,
        1 << 30,
    )(place, m, t, z0, above, below, cut, wr, ws)
    m = m[RIM : RIM + EXT] + summed(mine, theirs)
    t = across(m, 1)
    coded, out = call(
        third_kernel,
        [SMEM] + [VMEM] * 5,
        [f32(CH * ROWS, TW), f32(CH * ROWS, TW)],
        [bf16(EXT)] * 2,
        1 << 29,
    )(place, z1, m, t, cut, wr)
    return coded.reshape(CH, ROWS, TW), out.reshape(CH, ROWS, TW)


def solution(mesh):
    in_specs = (
        P(None, "tile", None),
        P("atom", "tile", None),
        P("atom", None, None, None),
        P("atom"),
    )
    out_specs = (P("atom", "tile", None), P(None, "tile", None))
    return jax.shard_map(
        per_device, mesh=mesh, in_specs=in_specs, out_specs=out_specs, check_vma=False
    )
```

```python
import jax
import jax.numpy as jnp
from jax import lax
from jax.experimental import pallas as pl
from jax.experimental.pallas import tpu as pltpu
from jax.sharding import PartitionSpec as P

STEP = 8.0
KS = 8
RIM = KS - 1
ROWS = 16
CH = 16
HALF = CH // 2
TW = 128
TAPS = KS * CH
EXT = ROWS + RIM
BUTTERFLY = (2, 4, 8, 24)


def split(x):
    hi = x.astype(jnp.bfloat16)
    lo = (x - hi.astype(jnp.float32)).astype(jnp.bfloat16)
    return hi, lo


def stacked(hi, lo):
    return jnp.concatenate(
        [jnp.concatenate([hi, hi], axis=1), jnp.concatenate([lo, lo], axis=1)], axis=0
    )


def weights(ref, turned=False):
    w = ref[...]
    return stacked(*split(w.T if turned else w))


def products(w, sources, count, backwards=False):
    half = w.shape[0] // 2
    for i in range(0, count, 2):
        pair = min(2, count - i)
        window = [
            jnp.concatenate(
                [
                    ref[i + d + RIM - a] if backwards else ref[i + d + a]
                    for ref in sources
                    for a in range(KS)
                ],
                axis=0,
            )
            for d in range(pair)
        ]
        x = jnp.concatenate(window, axis=1) if pair == 2 else window[0]
        q = jnp.dot(w, x, preferred_element_type=jnp.float32)
        q = q[:half] + q[half:]
        for d in range(pair):
            yield q[:, d * TW : (d + 1) * TW]


def gathered(q, lane, right):
    total = q[:CH]
    for b in range(1, KS):
        part = pltpu.roll(q[b * CH : (b + 1) * CH], b if right else TW - b, 1)
        keep = lane >= b if right else lane < TW - b
        total = total + jnp.where(keep, part, 0.0)
    return total


def lanes():
    return lax.broadcasted_iota(jnp.int32, (CH, TW), 1)


def shrunk(moved, cut):
    return moved - jnp.clip(moved, -cut, cut)


def synthesize(w, sources, own, mine_ref, theirs_ref):
    lane = lanes()
    for i, q in enumerate(products(w, sources, EXT, True)):
        s = gathered(q, lane, True)
        mine_ref[i] = jnp.where(own, s[:HALF], s[HALF:])
        theirs_ref[i] = jnp.where(own, s[HALF:], s[:HALF])


def first_kernel(place_ref, z_ref, ws_ref, mine_ref, theirs_ref, hi_ref, lo_ref):
    zero = jnp.zeros((CH, TW), jnp.bfloat16)
    for r in range(ROWS + 2 * RIM):
        if RIM <= r < EXT:
            hi_ref[r], lo_ref[r] = split(z_ref[pl.ds(r - RIM, CH, stride=ROWS), :])
        else:
            hi_ref[r] = zero
            lo_ref[r] = zero
    synthesize(weights(ws_ref, True), [hi_ref, lo_ref], place_ref[2] == 0, mine_ref, theirs_ref)


def bands(own, m, t):
    return jnp.where(own, jnp.concatenate([m, t], axis=0), jnp.concatenate([t, m], axis=0))


def second_kernel(
    place_ref, m_ref, t_ref, z_ref, above_ref, below_ref, cut_ref, wr_ref, ws_ref,
    z1_ref, mine_ref, theirs_ref, mhi_ref, mlo_ref, hi_ref, lo_ref,
):
    tile, last = place_ref[0], place_ref[1]
    own = place_ref[2] == 0
    for r in range(ROWS + 3 * RIM):
        mhi_ref[r], mlo_ref[r] = split(bands(own, m_ref[r], t_ref[r]))
    lane = lanes()
    cut = cut_ref[...]
    for n, q in enumerate(products(weights(wr_ref), [mhi_ref, mlo_ref], ROWS + 2 * RIM)):
        i = n - RIM
        if i < 0:
            z = above_ref[n]
        elif i < ROWS:
            z = z_ref[pl.ds(i, CH, stride=ROWS), :]
        else:
            z = below_ref[i - ROWS]
        z = shrunk(z - STEP * gathered(q, lane, False), cut)
        if i < 0:
            z = jnp.where(tile > 0, z, 0.0)
        elif i >= ROWS:
            z = jnp.where(tile < last, z, 0.0)
        else:
            z1_ref[i] = z
        hi_ref[n], lo_ref[n] = split(z)
    synthesize(weights(ws_ref, True), [hi_ref, lo_ref], own, mine_ref, theirs_ref)


def third_kernel(
    place_ref, z_ref, m_ref, t_ref, cut_ref, wr_ref, coded_ref, misfit_ref,
    hi_ref, lo_ref, out_ref, rows_ref, sems,
):
    lane = lanes()
    cut = cut_ref[...]
    own = place_ref[2] == 0
    inside = place_ref[0] < place_ref[1]
    for i in range(EXT):
        both = bands(own, m_ref[i], t_ref[i])
        if i < ROWS:
            out_ref[pl.ds(i, CH, stride=ROWS), :] = both
        else:
            both = jnp.where(inside, both, 0.0)
        hi_ref[i], lo_ref[i] = split(both)
    copies = [pltpu.make_async_copy(out_ref, misfit_ref, sems.at[0])]
    copies[0].start()
    for i, q in enumerate(products(weights(wr_ref), [hi_ref, lo_ref], ROWS)):
        z = shrunk(z_ref[i] - STEP * gathered(q, lane, False), cut)
        part, row = divmod(i, 8)
        rows_ref.at[part].reshape(CH * 8, TW)[pl.ds(row, CH, stride=8), :] = z
        if row == 7:
            copies.append(
                pltpu.make_async_copy(
                    rows_ref.at[part], coded_ref.at[:, part], sems.at[1 + part]
                )
            )
            copies[-1].start()
    for copy in copies:
        copy.wait()


VMEM = pl.BlockSpec(memory_space=pltpu.VMEM)
SMEM = pl.BlockSpec(memory_space=pltpu.SMEM)


def f32(*shape):
    return jax.ShapeDtypeStruct(shape, jnp.float32)


def bf16(rows):
    return pltpu.VMEM((rows, CH, TW), jnp.bfloat16)


def call(kernel, in_specs, outs, scratch, flops, place=None):
    return pl.pallas_call(
        kernel,
        in_specs=in_specs,
        out_specs=[place or VMEM] * len(outs),
        out_shape=outs,
        scratch_shapes=scratch,
        compiler_params=pltpu.CompilerParams(vmem_limit_bytes=16 << 20),
        cost_estimate=pl.CostEstimate(
            flops=flops, bytes_accessed=1 << 20, transcendentals=0
        ),
    )


def across(x, mask):
    n = lax.axis_size("atom")
    return lax.ppermute(x, "atom", [(i, i ^ mask) for i in range(n)])


def shifted(x, by):
    n = lax.axis_size("tile")
    return lax.ppermute(x, "tile", [(t, t + by) for t in range(n) if 0 <= t + by < n])


def summed(mine, theirs):
    total = mine + across(theirs, 1)
    for mask in BUTTERFLY:
        total = total + across(total, mask)
    return total


def flat(x):
    return x.reshape(-1, TW)


def per_device(observed, coefficients, dictionary, thresholds):
    core = lax.axis_index("atom") % 2
    tile = lax.axis_index("tile")
    last = lax.axis_size("tile") - 1
    place = jnp.stack([tile, jnp.full_like(tile, last), core]).astype(jnp.int32)
    z0 = flat(coefficients)
    ws = jnp.transpose(dictionary, (2, 0, 3, 1)).reshape(TAPS, TAPS)
    wr = jnp.transpose(dictionary, (3, 0, 2, 1)).reshape(TAPS, TAPS)
    cut = jnp.broadcast_to((STEP * thresholds)[:, None], (CH, TW))
    obs = jnp.transpose(
        jnp.where(core == 0, observed[:HALF], observed[HALF:]), (1, 0, 2)
    )
    part = f32(EXT, HALF, TW)

    mine, theirs = call(
        first_kernel,
        [SMEM, VMEM, VMEM],
        [part, part],
        [bf16(ROWS + 2 * RIM)] * 2,
        1 << 29,
    )(place, z0, ws)
    total = summed(mine, theirs)
    inner = total[:ROWS] - obs
    outer = total[ROWS:]
    top = jnp.transpose(coefficients[:, :RIM], (1, 0, 2))
    bottom = jnp.transpose(coefficients[:, ROWS - RIM :], (1, 0, 2))
    up = shifted(
        jnp.concatenate([flat(inner[: 2 * RIM]), flat(obs[:RIM]), flat(top)], axis=0), -1
    )
    down = shifted(
        jnp.concatenate([flat(inner[ROWS - RIM :]), flat(outer), flat(bottom)], axis=0), 1
    )
    side = RIM * HALF
    above_misfit = down[:side].reshape(RIM, HALF, TW)
    above_adds = down[side : 2 * side].reshape(RIM, HALF, TW)
    above = down[2 * side :].reshape(RIM, CH, TW)
    below_misfit = up[: 2 * side].reshape(2 * RIM, HALF, TW)
    obs_below = up[2 * side : 3 * side].reshape(RIM, HALF, TW)
    below = up[3 * side :].reshape(RIM, CH, TW)
    m = jnp.concatenate(
        [
            above_misfit,
            inner[:RIM] + above_adds,
            inner[RIM:],
            jnp.where(tile < last, below_misfit[:RIM] + outer, 0.0),
            below_misfit[RIM:],
        ],
        axis=0,
    )
    t = across(m, 1)
    z1, mine, theirs = call(
        second_kernel,
        [SMEM] + [VMEM] * 8,
        [f32(ROWS, CH, TW), part, part],
        [bf16(ROWS + 3 * RIM)] * 2 + [bf16(ROWS + 2 * RIM)] * 2,
        1 << 30,
    )(place, m, t, z0, above, below, cut, wr, ws)
    m = summed(mine, theirs) - jnp.concatenate([obs, obs_below], axis=0)
    t = across(m, 1)
    coded, out = call(
        third_kernel,
        [SMEM] + [VMEM] * 5,
        [f32(CH, 2, 8, TW), f32(CH * ROWS, TW)],
        [bf16(EXT)] * 2
        + [
            pltpu.VMEM((CH * ROWS, TW), jnp.float32),
            pltpu.VMEM((2, CH, 8, TW), jnp.float32),
            pltpu.SemaphoreType.DMA((3,)),
        ],
        1 << 29,
        pl.BlockSpec(memory_space=pl.ANY),
    )(place, z1, m, t, cut, wr)
    return coded.reshape(CH, ROWS, TW), out.reshape(CH, ROWS, TW)


def solution(mesh):
    in_specs = (
        P(None, "tile", None),
        P("atom", "tile", None),
        P("atom", None, None, None),
        P("atom"),
    )
    out_specs = (P("atom", "tile", None), P(None, "tile", None))
    return jax.shard_map(
        per_device, mesh=mesh, in_specs=in_specs, out_specs=out_specs, check_vma=False
    )
```
